32 devices in a mesh: node: 8 (over z, x), feat: 4 (over y, core).
Axes of the slice: x: 2, y: 2, z: 4, core: 2. Of those that a mesh axis runs over, the one named last changes fastest.
Arguments:
- features: bfloat16 [256, 4096], P('feat', 'node'), may hold values from -6 to 6
- tile_values: bfloat16 [256, 128, 128], P('node'), may hold values from -0.1875 to 0.1875
- tile_rows: int32 [64, 4], P('node'), may hold values from 0 to 3
- tile_cols: int32 [64, 4], P('node'), may hold values from 0 to 3
- tile_counts: int32 [64], P('node'), may hold values from 0 to 4, as said below
- weight: bfloat16 [256, 256], replicated, may hold values from -0.375 to 0.375
- cotangent: bfloat16 [256, 4096], P(None, ('node', 'feat')), may hold values from -6 to 6
Outputs:
- activated: bfloat16 [256, 4096], P(None, ('node', 'feat'))
- grad_weight: float32 [256, 256], replicated
- grad_features: float32 [256, 4096], P('feat', 'node')
The draws below stay inside these ranges and needn't reach their ends.
Inputs may be any that keep to these rules, and one draw needn't show every extreme that they name: `tile_counts`: slots at or past a pair's count are ignored; some pair has all 4 slots live, and the live slots of one receiving node index vary strongly between indices.
All inputs are finite; a program needn't handle non-finite values.
Results may differ from the reference program's by a relative error of at most 0.012.
Values may be sent and summed in bfloat16 or wider, within the bound.
No kernel may reach another device: no remote copies, remote signals or barrier semaphores. Data moves between devices by JAX's collectives and lax.ppermute only.
A program may use at most 64 MiB of HBM per device.

```python
import jax
import jax.numpy as jnp
from jax import lax

H = 256
TILE = 128
RB_DEV = 4
SLOT = 4
NODES = 4096
PAIRS = 64
TILES = 256
N_NODE = 8


def draw_tile_counts(key, part):
    level = jax.random.randint(jax.random.fold_in(key, 11), (N_NODE,), 1, SLOT + 1)
    level = jnp.where(jnp.arange(N_NODE) == 0, SLOT, level)
    drops = jax.random.randint(jax.random.fold_in(key, 12), (N_NODE * N_NODE,), 0, 2)
    drops = jnp.where(jnp.arange(N_NODE * N_NODE) == 0, 0, drops)
    counts = jnp.repeat(level, N_NODE) - drops
    return jnp.maximum(counts, 0).astype(jnp.int32)


def with_ends(array, own_key, least, top_value):
    dims = array.shape
    spot = [jax.random.randint(jax.random.fold_in(own_key, axis), (), 0, dims[axis]) for axis in range(len(dims))]
    array = array.at[tuple(spot)].set(least)
    longest = dims.index(max(dims))
    spot[longest] = (spot[longest] + 1) % dims[longest]
    return array.at[tuple(spot)].set(top_value)


def block_levels(stream_key, extent, cuts, least, largest):
    loudness = 1.0
    for axis_at, parts in cuts:
        heights = jax.random.uniform(jax.random.fold_in(jax.random.fold_in(stream_key, 6), axis_at), (parts,), jnp.float32, least / len(cuts), largest / len(cuts))
        loudness = loudness * jnp.repeat(jnp.exp(heights), extent[axis_at] // parts).reshape((-1,) + (1,) * (len(extent) - 1 - axis_at))
    return loudness


def gaussian(stream_key, dims, width, most, pieces=(), kind=jnp.bfloat16):
    gain = block_levels(stream_key, dims, pieces, -0.22, 0.18) if pieces else 1.0
    result = jax.random.normal(stream_key, dims, jnp.float32) * width * gain
    return jnp.minimum(jnp.maximum(result, -most), most).astype(kind)


def setup_inputs(seed: int = 0) -> dict:
    streams_of = jax.random.split(jax.random.key(seed), 8)
    features = gaussian(streams_of[0], (H, NODES), 1.0, 6.0, ((0, 4), (1, 8)))
    tile_values = gaussian(streams_of[1], (TILES, TILE, TILE), (TILE * SLOT * N_NODE // RB_DEV) ** -0.5, 0.1875, ((0, 8),))
    tile_rows = with_ends(jax.random.randint(streams_of[2], (PAIRS, SLOT), 0, RB_DEV), jax.random.fold_in(streams_of[2], 1), 0, RB_DEV - 1).astype(jnp.int32)
    tile_cols = with_ends(jax.random.randint(streams_of[3], (PAIRS, SLOT), 0, RB_DEV), jax.random.fold_in(streams_of[3], 1), 0, RB_DEV - 1).astype(jnp.int32)
    tile_counts = draw_tile_counts(jax.random.fold_in(streams_of[7], 71), 0)
    weight = gaussian(streams_of[5], (H, H), H ** -0.5, 0.375)
    cotangent = gaussian(streams_of[6], (H, NODES), 1.0, 6.0, ((1, 32),))
    return dict(features=features, tile_values=tile_values, tile_rows=tile_rows, tile_cols=tile_cols, tile_counts=tile_counts, weight=weight, cotangent=cotangent)


def reference(features, tile_values, tile_rows, tile_cols, tile_counts, weight, cotangent):
    blocks_all = N_NODE * RB_DEV
    feats = features.astype(jnp.float32).reshape(H, blocks_all, TILE)
    values = tile_values.reshape(N_NODE, N_NODE * SLOT, TILE, TILE)
    row_ids = tile_rows.reshape(N_NODE, N_NODE * SLOT)
    col_ids = tile_cols.reshape(N_NODE, N_NODE * SLOT)
    live = (jnp.arange(SLOT)[None, None, :] < tile_counts.reshape(N_NODE, N_NODE)[:, :, None])
    live = live.astype(jnp.float32).reshape(N_NODE, N_NODE * SLOT)
    sender = jnp.repeat(jnp.arange(N_NODE, dtype=jnp.int32), SLOT)

    def forward_one(inputs):
        tiles, rows_here, cols_here, live_here = inputs
        global_cols = (sender * RB_DEV + cols_here).astype(jnp.int32)
        blocks = feats[:, global_cols, :]
        product = jnp.einsum('hsm,sjm->hsj', blocks, tiles.astype(jnp.float32))
        place = jax.nn.one_hot(rows_here, RB_DEV, dtype=jnp.float32) * live_here[:, None]
        return jnp.einsum('hsj,sr->hrj', product, place)

    gathered = lax.map(forward_one, (values, row_ids, col_ids, live))
    aggregated = jnp.transpose(gathered, (1, 0, 2, 3)).reshape(H, NODES).astype(jnp.bfloat16)
    pre = jnp.dot(weight.T, aggregated, preferred_element_type=jnp.float32)
    activated = jax.nn.silu(pre).astype(jnp.bfloat16)
    sigma = jax.nn.sigmoid(pre)
    dpre = (cotangent.astype(jnp.float32) * sigma * (1.0 + pre * (1.0 - sigma))).astype(jnp.bfloat16)
    grad_weight = jnp.dot(aggregated, dpre.T, preferred_element_type=jnp.float32)
    dagg = jnp.dot(weight, dpre, preferred_element_type=jnp.float32).astype(jnp.bfloat16)
    dagg_blocks = jnp.transpose(dagg.astype(jnp.float32).reshape(H, N_NODE, RB_DEV, TILE), (1, 0, 2, 3))

    def backward_one(total, inputs):
        grads_here, tiles, rows_here, cols_here, live_here = inputs
        global_cols = (sender * RB_DEV + cols_here).astype(jnp.int32)
        pick = jax.nn.one_hot(rows_here, RB_DEV, dtype=jnp.float32)
        blocks = jnp.einsum('hrj,sr->hsj', grads_here, pick)
        product = jnp.einsum('hsj,sjm->hsm', blocks, tiles.astype(jnp.float32)) * live_here[None, :, None]
        return total.at[:, global_cols, :].add(product), None

    start = jnp.zeros((H, blocks_all, TILE), jnp.float32)
    total, _ = lax.scan(backward_one, start, (dagg_blocks, values, row_ids, col_ids, live))
    return activated, grad_weight, total.reshape(H, NODES)
```

```python
import functools

import jax
import jax.numpy as jnp
from jax import lax
from jax.experimental import pallas as pl
from jax.experimental.pallas import tpu as pltpu
from jax.sharding import PartitionSpec as P

BF16 = jnp.bfloat16
F32 = jnp.float32
SMEM = pl.BlockSpec(memory_space=pltpu.SMEM)
VMEM = pl.BlockSpec(memory_space=pltpu.VMEM)


def swapped(x, axis, mask):
    return lax.ppermute(x, axis, [(i, i ^ mask) for i in range(lax.axis_size(axis))])


def dot(a, b, dims):
    return lax.dot_general(a, b, (dims, ((), ())), preferred_element_type=F32)


def each(count, body):
    if count <= 8:
        for k in range(count):
            body(k)
    else:

        def step(k, carry):
            body(k)
            return carry

        lax.fori_loop(0, count, step, 0)


def lanes(block, side):
    start = block * side
    return pl.ds(start if isinstance(start, int) else pl.multiple_of(start, side), side)


def tree_sum(terms):
    while len(terms) > 1:
        terms = [a + b for a, b in zip(terms[::2], terms[1::2])]
    return terms[0]


def call(body, inputs, outputs, scratch=()):
    scalars = sum(1 for x in inputs if x.dtype == jnp.int32)
    held = sum(x.size * x.dtype.itemsize for x in [*inputs, *outputs])
    return pl.pallas_call(
        body,
        in_specs=[SMEM] * scalars + [VMEM] * (len(inputs) - scalars),
        out_specs=[VMEM] * len(outputs),
        out_shape=list(outputs),
        scratch_shapes=list(scratch),
        compiler_params=pltpu.CompilerParams(vmem_limit_bytes=2 * held + (8 << 20)),
    )(*inputs)


def add_forward(rows, cols, counts, values, pieces, totals, flip):
    own = lax.axis_index("node") ^ flip
    slots = rows.shape[1]
    side = values.shape[1]
    dummy = totals.shape[0] - 1

    def one(k):
        source = own ^ (2 * k)
        for slot in range(slots):
            block = pieces[k, :, lanes(cols[source, slot], side)]
            product = dot(block, values[source * slots + slot], ((1,), (1,)))
            to = jnp.where(slot < counts[source], rows[source, slot], dummy)
            totals[to] += product

    each(pieces.shape[0], one)


def add_backward(rows, cols, counts, values, grads, partial, store, flip, count):
    own = lax.axis_index("node") ^ flip
    slots = rows.shape[1]
    side = values.shape[1]
    dummy = partial.shape[0] - 1

    def one(k):
        owner = own ^ (2 * k)
        partial[...] = jnp.zeros_like(partial)
        for slot in range(slots):
            block = grads[:, lanes(rows[owner, slot], side)]
            product = dot(block, values[owner * slots + slot], ((1,), (0,)))
            to = jnp.where(slot < counts[owner], cols[owner, slot], dummy)
            partial[to] += product
        store(k, partial)

    each(count, one)


def forward_near(rows, cols, counts, values, pieces, totals):
    totals[...] = jnp.zeros_like(totals)
    add_forward(rows, cols, counts, values, pieces, totals, 0)


def forward_far(rows, cols, counts, values, pieces, near, out, totals):
    totals[...] = near[...]
    add_forward(rows, cols, counts, values, pieces, totals, 1)
    side = values.shape[1]
    for r in range(out.shape[1] // side):
        out[:, r * side : (r + 1) * side] = totals[r].astype(BF16)


def middle(rows, cols, counts, values, weight, *refs, feat):
    aggs, cots = refs[:feat], refs[feat : 2 * feat]
    activated, grads, sent, kept_weight, agg_full, dpre_full, partial = refs[2 * feat :]
    index = lax.axis_index("feat")
    width, local = aggs[0].shape
    side = cots[0].shape[1]
    for m in range(feat):
        agg_full[lanes(index ^ m, width), :] = aggs[m][...]
    for m in range(feat):
        at = lanes(index ^ m, side)
        pre = dot(weight[...], agg_full[:, at], ((0,), (0,)))
        sigma = 1.0 / (1.0 + jnp.exp(-pre))
        if m == 0:
            activated[...] = (pre * sigma).astype(BF16)
        dpre = cots[m][...].astype(F32) * sigma * (1.0 + pre * (1.0 - sigma))
        dpre_full[:, at] = dpre.astype(BF16)
    dpre_all = dpre_full[...]
    grads[...] = dot(weight[lanes(index, width), :], dpre_all, ((1,), (0,))).astype(BF16)
    weight_part = dot(aggs[0][...], dpre_all, ((1,), (1,))).astype(BF16)
    count = (sent.shape[0] - kept_weight.shape[0]) // width
    fold = kept_weight.shape[0]
    wide = weight_part.shape[1]
    for part in range(width // fold):
        piece = weight_part[part * fold : (part + 1) * fold]
        kept_weight[:, part * wide : (part + 1) * wide] = piece
        sent[count * width :, part * wide : (part + 1) * wide] = piece

    def store(k, partial):
        for c in range(local // side):
            sent[lanes(k, width), c * side : (c + 1) * side] = partial[c].astype(BF16)

    add_backward(rows, cols, counts, values, grads, partial, store, 1, count)


def backward_near(rows, cols, counts, values, grads, out, partial):
    width, local = grads.shape
    side = values.shape[1]

    def store(k, partial):
        for c in range(local // side):
            out[lanes(k, width), c * side : (c + 1) * side] = partial[c]

    add_backward(rows, cols, counts, values, grads, partial, store, 0, out.shape[0] // width)


def add_pair(near, got, kept_weight, own, own_weight, *sent):
    width = own.shape[0]
    total_weight = kept_weight[...].astype(F32) + got[near.shape[0] :, :].astype(F32)
    own_weight[...] = total_weight.astype(BF16)
    own[...] = near[:width] + got[:width].astype(F32)
    for k, out in enumerate(sent, 1):
        rows = slice(k * width, (k + 1) * width)
        out[:width] = (near[rows] + got[rows].astype(F32)).astype(BF16)
        out[width:] = total_weight.astype(BF16)


def add_column(own, own_weight, *refs):
    got, (gradient, weight_slice) = refs[:-2], refs[-2:]
    width = own.shape[0]
    gradient[...] = tree_sum([own[...]] + [g[:width].astype(F32) for g in got])
    weights = tree_sum([own_weight[...].astype(F32)] + [g[width:].astype(F32) for g in got])
    fold = weights.shape[0]
    wide = weight_slice.shape[1]
    for part in range(width // fold):
        piece = weights[:, part * wide : (part + 1) * wide]
        weight_slice[part * fold : (part + 1) * fold, :] = piece.astype(BF16)


def lay_out(*refs):
    slices, out = refs[:-1], refs[-1]
    index = lax.axis_index("feat")
    width = slices[0].shape[0]
    for m, piece in enumerate(slices):
        out[lanes(index ^ m, width), :] = piece[...].astype(F32)


def per_device(features, tile_values, tile_rows, tile_cols, tile_counts, weight, cotangent):
    nodes = lax.axis_size("node")
    feat = lax.axis_size("feat")
    column = nodes // 2
    width, local = features.shape
    wide = weight.shape[0]
    side = tile_values.shape[1]
    blocks = local // side
    fold = width * wide // local
    meta = (tile_rows, tile_cols, tile_counts, tile_values)
    shape = jax.ShapeDtypeStruct
    totals = (blocks + 1, width, side)

    pieces = [features] + [swapped(features, "node", 2 * k) for k in range(1, column)]
    pieces = jnp.stack(pieces)
    far_pieces = swapped(pieces, "node", 1)
    cots = [cotangent] + [swapped(cotangent, "feat", m) for m in range(1, feat)]
    (near,) = call(forward_near, [*meta, pieces], [shape(totals, F32)])
    (aggregated,) = call(
        forward_far,
        [*meta, far_pieces, near],
        [shape((width, local), BF16)],
        [pltpu.VMEM(totals, F32)],
    )
    aggs = [aggregated] + [swapped(aggregated, "feat", m) for m in range(1, feat)]
    activated, grads, sent, kept_weight = call(
        functools.partial(middle, feat=feat),
        [*meta, weight, *aggs, *cots],
        [
            shape((wide, side), BF16),
            shape((width, local), BF16),
            shape((column * width + fold, local), BF16),
            shape((fold, local), BF16),
        ],
        [
            pltpu.VMEM((wide, local), BF16),
            pltpu.VMEM((wide, local), BF16),
            pltpu.VMEM(totals, F32),
        ],
    )
    got = swapped(sent, "node", 1)
    (near_grads,) = call(
        backward_near,
        [*meta, grads],
        [shape((column * width, local), F32)],
        [pltpu.VMEM(totals, F32)],
    )
    own, own_weight, *chunks = call(
        add_pair,
        [near_grads, got, kept_weight],
        [shape((width, local), F32), shape((fold, local), BF16)]
        + [shape((width + fold, local), BF16)] * (column - 1),
    )
    arrived = [swapped(c, "node", 2 * k) for k, c in enumerate(chunks, 1)]
    gradient, weight_slice = call(
        add_column,
        [own, own_weight, *arrived],
        [shape((width, local), F32), shape((width, wide), BF16)],
    )
    slices = [weight_slice] + [swapped(weight_slice, "feat", m) for m in range(1, feat)]
    (grad_weight,) = call(lay_out, slices, [shape((wide, wide), F32)])
    return (activated, grad_weight, gradient)


def solution(mesh):
    placed = (
        P("feat", "node"),
        P("node", None, None),
        P("node", None),
        P("node", None),
        P("node"),
        P(),
        P(None, ("node", "feat")),
    )
    return jax.shard_map(
        per_device,
        mesh=mesh,
        in_specs=placed,
        out_specs=(P(None, ("node", "feat")), P(), P("feat", "node")),
        check_vma=False,
    )
```

```python
import functools

import jax
import jax.numpy as jnp
from jax import lax
from jax.experimental import pallas as pl
from jax.experimental.pallas import tpu as pltpu
from jax.sharding import PartitionSpec as P

BF16 = jnp.bfloat16
F32 = jnp.float32
SMEM = pl.BlockSpec(memory_space=pltpu.SMEM)
VMEM = pl.BlockSpec(memory_space=pltpu.VMEM)


def swapped(x, axis, mask):
    return lax.ppermute(x, axis, [(i, i ^ mask) for i in range(lax.axis_size(axis))])


def dot(a, b, dims):
    return lax.dot_general(a, b, (dims, ((), ())), preferred_element_type=F32)


def each(count, body):
    if count <= 8:
        for k in range(count):
            body(k)
    else:

        def step(k, carry):
            body(k)
            return carry

        lax.fori_loop(0, count, step, 0)


def lanes(block, side):
    start = block * side
    return pl.ds(start if isinstance(start, int) else pl.multiple_of(start, side), side)


def tree_sum(terms):
    while len(terms) > 1:
        terms = [a + b for a, b in zip(terms[::2], terms[1::2])]
    return terms[0]


def call(body, inputs, outputs, scratch=()):
    scalars = sum(1 for x in inputs if x.dtype == jnp.int32)
    held = sum(x.size * x.dtype.itemsize for x in [*inputs, *outputs])
    return pl.pallas_call(
        body,
        in_specs=[SMEM] * scalars + [VMEM] * (len(inputs) - scalars),
        out_specs=[VMEM] * len(outputs),
        out_shape=list(outputs),
        scratch_shapes=list(scratch),
        compiler_params=pltpu.CompilerParams(vmem_limit_bytes=2 * held + (8 << 20)),
    )(*inputs)


def add_forward(rows, cols, counts, values, pieces, totals, flip):
    own = lax.axis_index("node") ^ flip
    slots = rows.shape[1]
    side = values.shape[1]
    dummy = totals.shape[0] - 1

    def one(k):
        source = own ^ (2 * k)
        for slot in range(slots):
            block = pieces[k, :, lanes(cols[source, slot], side)]
            product = dot(block, values[source * slots + slot], ((1,), (1,)))
            to = jnp.where(slot < counts[source], rows[source, slot], dummy)
            totals[to] += product

    each(pieces.shape[0], one)


def add_backward(rows, cols, counts, values, grads, partial, store, flip, count):
    own = lax.axis_index("node") ^ flip
    slots = rows.shape[1]
    side = values.shape[1]
    dummy = partial.shape[0] - 1

    def one(k):
        owner = own ^ (2 * k)
        partial[...] = jnp.zeros_like(partial)
        for slot in range(slots):
            block = grads[:, lanes(rows[owner, slot], side)]
            product = dot(block, values[owner * slots + slot], ((1,), (0,)))
            to = jnp.where(slot < counts[owner], cols[owner, slot], dummy)
            partial[to] += product
        store(k, partial)

    each(count, one)


def forward_near(rows, cols, counts, values, pieces, totals):
    totals[...] = jnp.zeros_like(totals)
    add_forward(rows, cols, counts, values, pieces, totals, 0)


def forward_far(rows, cols, counts, values, pieces, near, out, totals):
    totals[...] = near[...]
    add_forward(rows, cols, counts, values, pieces, totals, 1)
    side = values.shape[1]
    for r in range(out.shape[1] // side):
        out[:, r * side : (r + 1) * side] = totals[r].astype(BF16)


def gather_feat(x):
    far = [swapped(x, "feat", m) for m in range(2, lax.axis_size("feat"), 2)]
    held = []
    for piece in [x, *far]:
        held += [piece, swapped(piece, "feat", 1)]
    return held


def stack(*refs):
    pieces, out = refs[:-1], refs[-1]
    for k, piece in enumerate(pieces):
        out[k] = piece[...]


def middle(rows, cols, counts, values, weight, *refs, feat):
    aggs, cots = refs[:feat], refs[feat : 2 * feat]
    activated, grads, sent, weight_part, agg_full, dpre_full, partial = refs[2 * feat :]
    index = lax.axis_index("feat")
    width, local = aggs[0].shape
    side = cots[0].shape[1]
    for m in range(feat):
        agg_full[lanes(index ^ m, width), :] = aggs[m][...]
    for m in range(feat):
        at = lanes(index ^ m, side)
        pre = dot(weight[...], agg_full[:, at], ((0,), (0,)))
        sigma = 1.0 / (1.0 + jnp.exp(-pre))
        if m == 0:
            activated[...] = (pre * sigma).astype(BF16)
        dpre = cots[m][...].astype(F32) * sigma * (1.0 + pre * (1.0 - sigma))
        dpre_full[:, at] = dpre.astype(BF16)
    dpre_all = dpre_full[...]
    grads[...] = dot(weight[lanes(index, width), :], dpre_all, ((1,), (0,))).astype(BF16)
    mine = agg_full[lanes(index & 1, weight_part.shape[0]), :]
    weight_part[...] = dot(mine, dpre_all, ((1,), (1,))).astype(BF16)

    def store(k, partial):
        for c in range(local // side):
            sent[lanes(k, width), c * side : (c + 1) * side] = partial[c].astype(BF16)

    add_backward(
        rows, cols, counts, values, grads, partial, store, 1, sent.shape[0] // width
    )


def backward_near(rows, cols, counts, values, grads, out, partial):
    width, local = grads.shape
    side = values.shape[1]

    def store(k, partial):
        for c in range(local // side):
            out[lanes(k, width), c * side : (c + 1) * side] = partial[c]

    add_backward(rows, cols, counts, values, grads, partial, store, 0, out.shape[0] // width)


def add_weights(one, other, out):
    out[...] = (one[...].astype(F32) + other[...].astype(F32)).astype(BF16)


def sum_weights(*refs):
    refs[-1][...] = tree_sum([r[...].astype(F32) for r in refs[:-1]])


def lay_out(mine, other, out):
    core = lax.axis_index("feat") & 1
    out[lanes(core, mine.shape[0]), :] = mine[...]
    out[lanes(core ^ 1, mine.shape[0]), :] = other[...]


def add_pair(near, got, own, *sent):
    width = own.shape[0]
    own[...] = near[:width] + got[:width].astype(F32)
    for k, out in enumerate(sent, 1):
        rows = slice(k * width, (k + 1) * width)
        out[...] = (near[rows] + got[rows].astype(F32)).astype(BF16)


def add_column(*refs):
    refs[-1][...] = tree_sum([r[...].astype(F32) for r in refs[:-1]])


def per_device(features, tile_values, tile_rows, tile_cols, tile_counts, weight, cotangent):
    nodes = lax.axis_size("node")
    feat = lax.axis_size("feat")
    column = nodes // 2
    width, local = features.shape
    wide = weight.shape[0]
    side = tile_values.shape[1]
    meta = (tile_rows, tile_cols, tile_counts, tile_values)
    shape = jax.ShapeDtypeStruct
    totals = (local // side + 1, width, side)

    pieces = [features] + [swapped(features, "node", 2 * k) for k in range(1, column)]
    (pieces,) = call(stack, pieces, [shape((column, width, local), BF16)])
    far_pieces = swapped(pieces, "node", 1)
    cots = gather_feat(cotangent)
    (near,) = call(forward_near, [*meta, pieces], [shape(totals, F32)])
    (aggregated,) = call(
        forward_far,
        [*meta, far_pieces, near],
        [shape((width, local), BF16)],
        [pltpu.VMEM(totals, F32)],
    )
    aggs = gather_feat(aggregated)
    activated, grads, sent, weight_part = call(
        functools.partial(middle, feat=feat),
        [*meta, weight, *aggs, *cots],
        [
            shape((wide, side), BF16),
            shape((width, local), BF16),
            shape((column * width, local), BF16),
            shape((wide // 2, wide), BF16),
        ],
        [
            pltpu.VMEM((wide, local), BF16),
            pltpu.VMEM((wide, local), BF16),
            pltpu.VMEM(totals, F32),
        ],
    )
    other_part = swapped(weight_part, "node", 1)
    got = swapped(sent, "node", 1)
    (near_grads,) = call(
        backward_near,
        [*meta, grads],
        [shape((column * width, local), F32)],
        [pltpu.VMEM(totals, F32)],
    )
    other_part, near_grads = lax.optimization_barrier((other_part, near_grads))
    (pair,) = call(add_weights, [weight_part, other_part], [shape((wide // 2, wide), BF16)])
    pairs = [pair] + [swapped(pair, "node", 2 * k) for k in range(1, column)]
    own, *chunks = call(
        add_pair,
        [near_grads, got],
        [shape((width, local), F32)] + [shape((width, local), BF16)] * (column - 1),
    )
    arrived = [swapped(c, "node", 2 * k) for k, c in enumerate(chunks, 1)]
    *pairs, _ = lax.optimization_barrier((*pairs, chunks[0]))
    (half,) = call(sum_weights, pairs, [shape((wide // 2, wide), F32)])
    other_half = swapped(half, "feat", 1)
    (grad_weight,) = call(lay_out, [half, other_half], [shape((wide, wide), F32)])
    *arrived, grad_weight = lax.optimization_barrier((*arrived, grad_weight))
    (gradient,) = call(add_column, [own, *arrived], [shape((width, local), F32)])
    return (activated, grad_weight, gradient)


def solution(mesh):
    placed = (
        P("feat", "node"),
        P("node", None, None),
        P("node", None),
        P("node", None),
        P("node"),
        P(),
        P(None, ("node", "feat")),
    )
    return jax.shard_map(
        per_device,
        mesh=mesh,
        in_specs=placed,
        out_specs=(P(None, ("node", "feat")), P(), P("feat", "node")),
        check_vma=False,
    )
```

```python
import functools

import jax
import jax.numpy as jnp
from jax import lax
from jax.experimental import pallas as pl
from jax.experimental.pallas import tpu as pltpu
from jax.sharding import PartitionSpec as P

BF16 = jnp.bfloat16
F32 = jnp.float32
SMEM = pl.BlockSpec(memory_space=pltpu.SMEM)
VMEM = pl.BlockSpec(memory_space=pltpu.VMEM)


def swapped(x, axis, mask):
    return lax.ppermute(x, axis, [(i, i ^ mask) for i in range(lax.axis_size(axis))])


def dot(a, b, dims):
    return lax.dot_general(a, b, (dims, ((), ())), preferred_element_type=F32)


def each(count, body):
    if count <= 8:
        for k in range(count):
            body(k)
    else:

        def step(k, carry):
            body(k)
            return carry

        lax.fori_loop(0, count, step, 0)


def lanes(block, side):
    start = block * side
    return pl.ds(start if isinstance(start, int) else pl.multiple_of(start, side), side)


def tree_sum(terms):
    while len(terms) > 1:
        terms = [a + b for a, b in zip(terms[::2], terms[1::2])]
    return terms[0]


def call(body, inputs, outputs, scratch=()):
    scalars = sum(1 for x in inputs if x.dtype == jnp.int32)
    held = sum(x.size * x.dtype.itemsize for x in [*inputs, *outputs])
    return pl.pallas_call(
        body,
        in_specs=[SMEM] * scalars + [VMEM] * (len(inputs) - scalars),
        out_specs=[VMEM] * len(outputs),
        out_shape=list(outputs),
        scratch_shapes=list(scratch),
        compiler_params=pltpu.CompilerParams(vmem_limit_bytes=2 * held + (8 << 20)),
    )(*inputs)


def add_forward(rows, cols, counts, values, first, rest, totals, flip):
    own = lax.axis_index("node") ^ flip
    slots = rows.shape[1]
    side = values.shape[1]
    dummy = totals.shape[0] - 1

    def one(k, piece):
        source = own ^ (2 * k)
        for slot in range(slots):
            block = piece[:, lanes(cols[source, slot], side)]
            product = dot(block, values[source * slots + slot], ((1,), (1,)))
            to = jnp.where(slot < counts[source], rows[source, slot], dummy)
            totals[to] += product

    one(0, first)
    each(rest.shape[0], lambda k: one(k + 1, rest.at[k]))


def add_backward(rows, cols, counts, values, grads, partial, store, flip, count):
    own = lax.axis_index("node") ^ flip
    slots = rows.shape[1]
    side = values.shape[1]
    dummy = partial.shape[0] - 1

    def one(k):
        owner = own ^ (2 * k)
        partial[...] = jnp.zeros_like(partial)
        for slot in range(slots):
            block = grads[:, lanes(rows[owner, slot], side)]
            product = dot(block, values[owner * slots + slot], ((1,), (0,)))
            to = jnp.where(slot < counts[owner], cols[owner, slot], dummy)
            partial[to] += product
        store(k, partial)

    each(count, one)


def forward_near(rows, cols, counts, values, first, rest, totals):
    totals[...] = jnp.zeros_like(totals)
    add_forward(rows, cols, counts, values, first, rest, totals, 0)


def forward_far(rows, cols, counts, values, first, rest, near, out, totals):
    totals[...] = near[...]
    add_forward(rows, cols, counts, values, first, rest, totals, 1)
    side = values.shape[1]
    for r in range(out.shape[1] // side):
        out[:, r * side : (r + 1) * side] = totals[r].astype(BF16)


def gather_feat(x):
    far = [swapped(x, "feat", m) for m in range(2, lax.axis_size("feat"), 2)]
    held = []
    for piece in [x, *far]:
        held += [piece, swapped(piece, "feat", 1)]
    return held


def stack(*refs):
    pieces, out = refs[:-1], refs[-1]
    for k, piece in enumerate(pieces):
        out[k] = piece[...]


def middle(weight, *refs, feat):
    aggs, cots = refs[:feat], refs[feat : 2 * feat]
    activated, grads, weight_part, agg_full, dpre_full = refs[2 * feat :]
    index = lax.axis_index("feat")
    width, local = aggs[0].shape
    side = cots[0].shape[1]
    for m in range(feat):
        agg_full[lanes(index ^ m, width), :] = aggs[m][...]
    for m in range(feat):
        at = lanes(index ^ m, side)
        pre = dot(weight[...], agg_full[:, at], ((0,), (0,)))
        sigma = 1.0 / (1.0 + jnp.exp(-pre))
        if m == 0:
            activated[...] = (pre * sigma).astype(BF16)
        dpre = cots[m][...].astype(F32) * sigma * (1.0 + pre * (1.0 - sigma))
        dpre_full[:, at] = dpre.astype(BF16)
    dpre_all = dpre_full[...]
    grads[...] = dot(weight[lanes(index, width), :], dpre_all, ((1,), (0,))).astype(BF16)
    mine = agg_full[lanes(index & 1, weight_part.shape[0]), :]
    weight_part[...] = dot(mine, dpre_all, ((1,), (1,))).astype(BF16)


def backward(rows, cols, counts, values, grads, out, partial, *, flip):
    width, local = grads.shape
    side = values.shape[1]

    def store(k, partial):
        for c in range(local // side):
            out[lanes(k, width), c * side : (c + 1) * side] = partial[c].astype(out.dtype)

    add_backward(
        rows, cols, counts, values, grads, partial, store, flip, out.shape[0] // width
    )


def add_weights(one, other, out):
    out[...] = (one[...].astype(F32) + other[...].astype(F32)).astype(BF16)


def sum_weights(*refs):
    refs[-1][...] = tree_sum([r[...].astype(F32) for r in refs[:-1]])


def lay_out(mine, other, out):
    core = lax.axis_index("feat") & 1
    out[lanes(core, mine.shape[0]), :] = mine[...]
    out[lanes(core ^ 1, mine.shape[0]), :] = other[...]


def add_pair(near, got, own, *sent):
    width = own.shape[0]
    own[...] = near[:width] + got[:width].astype(F32)
    for k, out in enumerate(sent, 1):
        rows = slice(k * width, (k + 1) * width)
        out[...] = (near[rows] + got[rows].astype(F32)).astype(BF16)


def add_column(*refs):
    refs[-1][...] = tree_sum([r[...].astype(F32) for r in refs[:-1]])


def per_device(features, tile_values, tile_rows, tile_cols, tile_counts, weight, cotangent):
    nodes = lax.axis_size("node")
    feat = lax.axis_size("feat")
    column = nodes // 2
    width, local = features.shape
    wide = weight.shape[0]
    side = tile_values.shape[1]
    meta = (tile_rows, tile_cols, tile_counts, tile_values)
    shape = jax.ShapeDtypeStruct
    totals = (local // side + 1, width, side)

    own_across = swapped(features, "node", 1)
    pieces = [swapped(features, "node", 2 * k) for k in range(1, column)]
    *pieces, own_across = lax.optimization_barrier((*pieces, own_across))
    (pieces,) = call(stack, pieces, [shape((column - 1, width, local), BF16)])
    far_pieces = swapped(pieces, "node", 1)
    cots = gather_feat(cotangent)
    (near,) = call(forward_near, [*meta, features, pieces], [shape(totals, F32)])
    (aggregated,) = call(
        forward_far,
        [*meta, own_across, far_pieces, near],
        [shape((width, local), BF16)],
        [pltpu.VMEM(totals, F32)],
    )
    aggs = gather_feat(aggregated)
    activated, grads, weight_part = call(
        functools.partial(middle, feat=feat),
        [weight, *aggs, *cots],
        [
            shape((wide, side), BF16),
            shape((width, local), BF16),
            shape((wide // 2, wide), BF16),
        ],
        [pltpu.VMEM((wide, local), BF16), pltpu.VMEM((wide, local), BF16)],
    )
    other_part = swapped(weight_part, "node", 1)
    (sent,) = call(
        functools.partial(backward, flip=1),
        [*meta, grads],
        [shape((column * width, local), BF16)],
        [pltpu.VMEM(totals, F32)],
    )
    (near_grads,) = call(
        functools.partial(backward, flip=0),
        [*meta, grads],
        [shape((column * width, local), F32)],
        [pltpu.VMEM(totals, F32)],
    )
    sent, near_grads, other_part = lax.optimization_barrier((sent, near_grads, other_part))
    got = swapped(sent, "node", 1)
    (pair,) = call(add_weights, [weight_part, other_part], [shape((wide // 2, wide), BF16)])
    pairs = [pair] + [swapped(pair, "node", 2 * k) for k in range(1, column)]
    own, *chunks = call(
        add_pair,
        [near_grads, got],
        [shape((width, local), F32)] + [shape((width, local), BF16)] * (column - 1),
    )
    arrived = [swapped(c, "node", 2 * k) for k, c in enumerate(chunks, 1)]
    *pairs, _ = lax.optimization_barrier((*pairs, chunks[0]))
    (half,) = call(sum_weights, pairs, [shape((wide // 2, wide), F32)])
    other_half = swapped(half, "feat", 1)
    (grad_weight,) = call(lay_out, [half, other_half], [shape((wide, wide), F32)])
    *arrived, grad_weight = lax.optimization_barrier((*arrived, grad_weight))
    (gradient,) = call(add_column, [own, *arrived], [shape((width, local), F32)])
    return (activated, grad_weight, gradient)


def solution(mesh):
    placed = (
        P("feat", "node"),
        P("node", None, None),
        P("node", None),
        P("node", None),
        P("node"),
        P(),
        P(None, ("node", "feat")),
    )
    return jax.shard_map(
        per_device,
        mesh=mesh,
        in_specs=placed,
        out_specs=(P(None, ("node", "feat")), P(), P("feat", "node")),
        check_vma=False,
    )
```

```python
import functools

import jax
import jax.numpy as jnp
from jax import lax
from jax.experimental import pallas as pl
from jax.experimental.pallas import tpu as pltpu
from jax.sharding import PartitionSpec as P

BF16 = jnp.bfloat16
F32 = jnp.float32
SMEM = pl.BlockSpec(memory_space=pltpu.SMEM)
VMEM = pl.BlockSpec(memory_space=pltpu.VMEM)
LARGE = pl.CostEstimate(flops=10**10, transcendentals=0, bytes_accessed=1 << 20)
SMALL = pl.CostEstimate(flops=1 << 10, transcendentals=0, bytes_accessed=1 << 10)


def swapped(x, axis, mask):
    return lax.ppermute(x, axis, [(i, i ^ mask) for i in range(lax.axis_size(axis))])


def dot(a, b, dims):
    return lax.dot_general(a, b, (dims, ((), ())), preferred_element_type=F32)


def each(count, body):
    if count <= 8:
        for k in range(count):
            body(k)
    else:

        def step(k, carry):
            body(k)
            return carry

        lax.fori_loop(0, count, step, 0)


def lanes(block, side):
    start = block * side
    return pl.ds(start if isinstance(start, int) else pl.multiple_of(start, side), side)


def tree_sum(terms):
    while len(terms) > 1:
        terms = [a + b for a, b in zip(terms[::2], terms[1::2])]
    return terms[0]


def call(body, inputs, outputs, scratch=(), cost=None, spec=VMEM):
    scalars = sum(1 for x in inputs if x.dtype == jnp.int32)
    held = sum(x.size * x.dtype.itemsize for x in [*inputs, *outputs])
    return pl.pallas_call(
        body,
        in_specs=[SMEM] * scalars + [spec] * (len(inputs) - scalars),
        out_specs=[VMEM] * len(outputs),
        out_shape=list(outputs),
        scratch_shapes=list(scratch),
        cost_estimate=cost,
        compiler_params=pltpu.CompilerParams(vmem_limit_bytes=2 * held + (8 << 20)),
    )(*inputs)


def prepare(rows, cols, counts, source, values, row_masks, col_masks, arrival):
    copy = pltpu.make_async_copy(source, values, arrival)
    copy.start()
    slots = rows.shape[0]
    shape = row_masks.shape[2:]

    def one(k):
        for slot in range(slots):
            live = slot < counts[k]
            for ids, masks in ((rows, row_masks), (cols, col_masks)):
                block = jnp.full(shape, jnp.where(live, ids[slot, k], -1), jnp.int32)
                for b in range(masks.shape[1]):
                    masks[k * slots + slot, b] = jnp.where(block == b, 1.0, 0.0).astype(BF16)

    each(rows.shape[1], one)
    copy.wait()


def tile_sums(values, pick, place, piece, pair, transposed):
    blocks = pick.shape[1]
    slots = values.shape[0] // lax.axis_size("node")
    side = values.shape[1]
    high = pick.shape[2]
    loaded = [piece[:, b * side : (b + 1) * side] for b in range(blocks)]
    fold = (-1, high, side)
    sums = [[] for _ in range(blocks)]
    for slot in range(slots):
        at = pair * slots + slot
        chosen = tree_sum([loaded[b].reshape(fold) * pick[at, b] for b in range(blocks)])
        chosen = chosen.reshape(loaded[0].shape)
        product = dot(chosen, values[at], ((1,), (1 if transposed else 0,))).reshape(fold)
        for b in range(blocks):
            sums[b].append(product * place[at, b].astype(F32))
    return [tree_sum(s).reshape(loaded[0].shape) for s in sums]


def forward_near(values, row_masks, col_masks, first, rest, across, totals):
    own = lax.axis_index("node")

    def one(k, piece):
        sums = tile_sums(values, col_masks, row_masks, piece, own ^ k, True)
        for r, part in enumerate(sums):
            totals[r] = part if piece is first else totals[r] + part

    one(0, first)
    one(1, across)
    each(rest.shape[0], lambda k: one(2 * k + 2, rest.at[k]))


def forward_far(values, row_masks, col_masks, rest, near, out, totals):
    own = lax.axis_index("node") ^ 1
    side = values.shape[1]
    totals[...] = near[...]

    def one(k):
        pair = own ^ (2 * k + 2)
        sums = tile_sums(values, col_masks, row_masks, rest.at[k], pair, True)
        for r, part in enumerate(sums):
            totals[r] += part

    each(rest.shape[0], one)
    for r in range(totals.shape[0]):
        out[:, r * side : (r + 1) * side] = totals[r].astype(BF16)


def add_backward(values, row_masks, col_masks, grads, out, flip):
    own = lax.axis_index("node") ^ flip
    width = grads.shape[0]
    side = values.shape[1]

    def one(k):
        sums = tile_sums(values, row_masks, col_masks, grads, own ^ (2 * k), False)
        for c, part in enumerate(sums):
            out[lanes(k, width), c * side : (c + 1) * side] = part.astype(out.dtype)

    each(out.shape[0] // width, one)


def gather_feat(x):
    far = [swapped(x, "feat", m) for m in range(2, lax.axis_size("feat"), 2)]
    held = []
    for piece in [x, *far]:
        held += [piece, swapped(piece, "feat", 1)]
    return held


def stack(*refs):
    pieces, out = refs[:-1], refs[-1]
    for k, piece in enumerate(pieces):
        out[k] = piece[...]


def middle(values, row_masks, col_masks, weight, *refs, feat):
    aggs, cots = refs[:feat], refs[feat : 2 * feat]
    activated, grads, weight_part, sent, agg_full, dpre_full = refs[2 * feat :]
    index = lax.axis_index("feat")
    width, local = aggs[0].shape
    side = cots[0].shape[1]
    for m in range(feat):
        agg_full[lanes(index ^ m, width), :] = aggs[m][...]
    for m in range(feat):
        at = lanes(index ^ m, side)
        pre = dot(weight[...], agg_full[:, at], ((0,), (0,)))
        sigma = 1.0 / (1.0 + jnp.exp(-pre))
        if m == 0:
            activated[...] = (pre * sigma).astype(BF16)
        dpre = cots[m][...].astype(F32) * sigma * (1.0 + pre * (1.0 - sigma))
        dpre_full[:, at] = dpre.astype(BF16)
    dpre_all = dpre_full[...]
    grads[...] = dot(weight[lanes(index, width), :], dpre_all, ((1,), (0,))).astype(BF16)
    mine = agg_full[lanes(index & 1, weight_part.shape[0]), :]
    weight_part[...] = dot(mine, dpre_all, ((1,), (1,))).astype(BF16)
    add_backward(values, row_masks, col_masks, grads, sent, 1)


def backward_near(values, row_masks, col_masks, grads, out):
    add_backward(values, row_masks, col_masks, grads, out, 0)


def add_weights(one, other, out):
    out[...] = (one[...].astype(F32) + other[...].astype(F32)).astype(BF16)


def sum_weights(*refs):
    refs[-1][...] = tree_sum([r[...].astype(F32) for r in refs[:-1]])


def lay_out(mine, other, activated, out, activated_out):
    activated_out[...] = activated[...]
    core = lax.axis_index("feat") & 1
    out[lanes(core, mine.shape[0]), :] = mine[...]
    out[lanes(core ^ 1, mine.shape[0]), :] = other[...]


def add_pair(near, got, own, *sent):
    width = own.shape[0]
    own[...] = near[:width] + got[:width].astype(F32)
    for k, out in enumerate(sent, 1):
        rows = slice(k * width, (k + 1) * width)
        out[...] = (near[rows] + got[rows].astype(F32)).astype(BF16)


def add_column(*refs):
    refs[-1][...] = tree_sum([r[...].astype(F32) for r in refs[:-1]])


def per_device(features, tile_values, tile_rows, tile_cols, tile_counts, weight, cotangent):
    nodes = lax.axis_size("node")
    feat = lax.axis_size("feat")
    column = nodes // 2
    width, local = features.shape
    wide = weight.shape[0]
    side = tile_values.shape[1]
    shape = jax.ShapeDtypeStruct
    totals = (local // side, width, side)

    own_across = swapped(features, "node", 1)
    pieces = [swapped(features, "node", 2 * k) for k in range(1, column)]
    masks = shape((tile_values.shape[0], local // side, 16, side), BF16)
    tiles = call(
        prepare,
        [tile_rows.T, tile_cols.T, tile_counts, tile_values],
        [shape(tile_values.shape, BF16), masks, masks],
        [pltpu.SemaphoreType.DMA],
        spec=pl.BlockSpec(memory_space=pltpu.HBM),
    )
    *pieces, own_across, t0, t1, t2 = lax.optimization_barrier((*pieces, own_across, *tiles))
    tiles = (t0, t1, t2)
    (pieces,) = call(stack, pieces, [shape((column - 1, width, local), BF16)])
    far_pieces = swapped(pieces, "node", 1)
    cots = gather_feat(cotangent)
    (near,) = call(
        forward_near, [*tiles, features, pieces, own_across], [shape(totals, F32)]
    )
    (aggregated,) = call(
        forward_far,
        [*tiles, far_pieces, near],
        [shape((width, local), BF16)],
        [pltpu.VMEM(totals, F32)],
    )
    aggs = gather_feat(aggregated)
    activated, grads, weight_part, sent = call(
        functools.partial(middle, feat=feat),
        [*tiles, weight, *aggs, *cots],
        [
            shape((wide, side), BF16),
            shape((width, local), BF16),
            shape((wide // 2, wide), BF16),
            shape((column * width, local), BF16),
        ],
        [pltpu.VMEM((wide, local), BF16), pltpu.VMEM((wide, local), BF16)],
    )
    other_part = swapped(weight_part, "node", 1)
    got = swapped(sent, "node", 1)
    (pair,) = call(
        add_weights, [weight_part, other_part], [shape((wide // 2, wide), BF16)], cost=SMALL
    )
    pair, grads = lax.optimization_barrier((pair, grads))
    (near_grads,) = call(
        backward_near,
        [*tiles, grads],
        [shape((column * width, local), F32)],
        cost=LARGE,
    )
    pairs = [pair] + [swapped(pair, "node", 2 * k) for k in range(1, column)]
    own, *chunks = call(
        add_pair,
        [near_grads, got],
        [shape((width, local), F32)] + [shape((width, local), BF16)] * (column - 1),
        cost=SMALL,
    )
    arrived = [swapped(c, "node", 2 * k) for k, c in enumerate(chunks, 1)]
    count = len(arrived)
    held = lax.optimization_barrier((*arrived, *pairs))
    arrived, pairs = held[:count], held[count:]
    (half,) = call(sum_weights, pairs, [shape((wide // 2, wide), F32)], cost=SMALL)
    other_half = swapped(half, "feat", 1)
    (gradient,) = call(
        add_column, [own, *arrived], [shape((width, local), F32)], cost=SMALL
    )
    grad_weight, activated = call(
        lay_out,
        [half, other_half, activated],
        [shape((wide, wide), F32), shape((wide, side), BF16)],
        cost=SMALL,
    )
    return (activated, grad_weight, gradient)


def solution(mesh):
    placed = (
        P("feat", "node"),
        P("node", None, None),
        P("node", None),
        P("node", None),
        P("node"),
        P(),
        P(None, ("node", "feat")),
    )
    return jax.shard_map(
        per_device,
        mesh=mesh,
        in_specs=placed,
        out_specs=(P(None, ("node", "feat")), P(), P("feat", "node")),
        check_vma=False,
    )
```

```python
import functools

import jax
import jax.numpy as jnp
from jax import lax
from jax.experimental import pallas as pl
from jax.experimental.pallas import tpu as pltpu
from jax.sharding import PartitionSpec as P

BF16 = jnp.bfloat16
F32 = jnp.float32
SMEM = pl.BlockSpec(memory_space=pltpu.SMEM)
VMEM = pl.BlockSpec(memory_space=pltpu.VMEM)
LARGE = pl.CostEstimate(flops=10**10, transcendentals=0, bytes_accessed=1 << 20)
SMALL = pl.CostEstimate(flops=1 << 10, transcendentals=0, bytes_accessed=1 << 10)


def swapped(x, axis, mask):
    return lax.ppermute(x, axis, [(i, i ^ mask) for i in range(lax.axis_size(axis))])


def dot(a, b, dims):
    return lax.dot_general(a, b, (dims, ((), ())), preferred_element_type=F32)


def each(count, body):
    if count <= 8:
        for k in range(count):
            body(k)
    else:

        def step(k, carry):
            body(k)
            return carry

        lax.fori_loop(0, count, step, 0)


def lanes(block, side):
    start = block * side
    return pl.ds(start if isinstance(start, int) else pl.multiple_of(start, side), side)


def tree_sum(terms):
    while len(terms) > 1:
        terms = [a + b for a, b in zip(terms[::2], terms[1::2])]
    return terms[0]


def call(body, inputs, outputs, scratch=(), cost=None, spec=VMEM):
    scalars = sum(1 for x in inputs if x.dtype == jnp.int32)
    held = sum(x.size * x.dtype.itemsize for x in [*inputs, *outputs])
    return pl.pallas_call(
        body,
        in_specs=[SMEM] * scalars + [spec] * (len(inputs) - scalars),
        out_specs=[VMEM] * len(outputs),
        out_shape=list(outputs),
        scratch_shapes=list(scratch),
        cost_estimate=cost,
        compiler_params=pltpu.CompilerParams(vmem_limit_bytes=2 * held + (8 << 20)),
    )(*inputs)


def prepare(rows, cols, counts, source, values, row_masks, col_masks, arrival):
    copy = pltpu.make_async_copy(source, values, arrival)
    copy.start()
    slots = rows.shape[0]
    shape = row_masks.shape[2:]

    def one(k):
        for slot in range(slots):
            live = slot < counts[k]
            for ids, masks in ((rows, row_masks), (cols, col_masks)):
                block = jnp.full(shape, jnp.where(live, ids[slot, k], -1), jnp.int32)
                for b in range(masks.shape[1]):
                    masks[k * slots + slot, b] = jnp.where(block == b, 1.0, 0.0).astype(BF16)

    each(rows.shape[1], one)
    copy.wait()


def tile_sums(values, pick, place, piece, pair, transposed):
    blocks = pick.shape[1]
    slots = values.shape[0] // lax.axis_size("node")
    side = values.shape[1]
    high = pick.shape[2]
    loaded = [piece[:, b * side : (b + 1) * side] for b in range(blocks)]
    fold = (-1, high, side)
    sums = [[] for _ in range(blocks)]
    for slot in range(slots):
        at = pair * slots + slot
        chosen = tree_sum([loaded[b].reshape(fold) * pick[at, b] for b in range(blocks)])
        chosen = chosen.reshape(loaded[0].shape)
        product = dot(chosen, values[at], ((1,), (1 if transposed else 0,))).reshape(fold)
        for b in range(blocks):
            sums[b].append(product * place[at, b].astype(F32))
    return [tree_sum(s).reshape(loaded[0].shape) for s in sums]


def forward_near(values, row_masks, col_masks, first, rest, across, totals):
    own = lax.axis_index("node")

    def one(k, piece):
        sums = tile_sums(values, col_masks, row_masks, piece, own ^ k, True)
        for r, part in enumerate(sums):
            totals[r] = part if piece is first else totals[r] + part

    one(0, first)
    one(1, across)
    each(rest.shape[0], lambda k: one(2 * k + 2, rest.at[k]))


def forward_far(values, row_masks, col_masks, rest, near, out, totals):
    own = lax.axis_index("node") ^ 1
    side = values.shape[1]
    totals[...] = near[...]

    def one(k):
        pair = own ^ (2 * k + 2)
        sums = tile_sums(values, col_masks, row_masks, rest.at[k], pair, True)
        for r, part in enumerate(sums):
            totals[r] += part

    each(rest.shape[0], one)
    for r in range(totals.shape[0]):
        out[:, r * side : (r + 1) * side] = totals[r].astype(BF16)


def add_backward(values, row_masks, col_masks, grads, out, flip):
    own = lax.axis_index("node") ^ flip
    width = grads.shape[0]
    side = values.shape[1]

    def one(k):
        sums = tile_sums(values, row_masks, col_masks, grads, own ^ (2 * k), False)
        for c, part in enumerate(sums):
            out[lanes(k, width), c * side : (c + 1) * side] = part.astype(out.dtype)

    each(out.shape[0] // width, one)


def gather_feat(x):
    far = [swapped(x, "feat", m) for m in range(2, lax.axis_size("feat"), 2)]
    held = []
    for piece in [x, *far]:
        held += [piece, swapped(piece, "feat", 1)]
    return held


def stack(*refs):
    pieces, out = refs[:-1], refs[-1]
    for k, piece in enumerate(pieces):
        out[k] = piece[...]


def middle(values, row_masks, col_masks, weight, *refs, feat):
    aggs, cots = refs[:feat], refs[feat : 2 * feat]
    activated, grads, mine, dpre_full, sent, agg_full = refs[2 * feat :]
    index = lax.axis_index("feat")
    width, local = aggs[0].shape
    side = cots[0].shape[1]
    for m in range(feat):
        agg_full[lanes(index ^ m, width), :] = aggs[m][...]
    for m in range(feat):
        at = lanes(index ^ m, side)
        pre = dot(weight[...], agg_full[:, at], ((0,), (0,)))
        sigma = 1.0 / (1.0 + jnp.exp(-pre))
        if m == 0:
            activated[...] = (pre * sigma).astype(BF16)
        dpre = cots[m][...].astype(F32) * sigma * (1.0 + pre * (1.0 - sigma))
        dpre_full[:, at] = dpre.astype(BF16)
    dpre_all = dpre_full[...]
    grads[...] = dot(weight[lanes(index, width), :], dpre_all, ((1,), (0,))).astype(BF16)
    mine[...] = agg_full[lanes(index & 1, mine.shape[0]), :]
    add_backward(values, row_masks, col_masks, grads, sent, 1)


def backward_near(values, row_masks, col_masks, grads, mine, dpre, out, weight_part):
    weight_part[...] = dot(mine[...], dpre[...], ((1,), (1,))).astype(BF16)
    add_backward(values, row_masks, col_masks, grads, out, 0)


def add_weights(one, other, out):
    out[...] = (one[...].astype(F32) + other[...].astype(F32)).astype(BF16)


def sum_weights(*refs):
    refs[-1][...] = tree_sum([r[...].astype(F32) for r in refs[:-1]]).astype(refs[-1].dtype)


def add_pair(near, got, own, *sent):
    width = own.shape[0]
    own[...] = near[:width] + got[:width].astype(F32)
    for k, out in enumerate(sent, 1):
        rows = slice(k * width, (k + 1) * width)
        out[...] = (near[rows] + got[rows].astype(F32)).astype(BF16)


def finish(activated, mine, other, column_sum, activated_out, weight_out, gradient):
    activated_out[...] = activated[...]
    core = lax.axis_index("feat") & 1
    weight_out[lanes(core, mine.shape[0]), :] = mine[...]
    weight_out[lanes(core ^ 1, mine.shape[0]), :] = other[...]
    gradient[...] = column_sum[...]


def add_column(*refs):
    refs[-1][...] = sum(r[...].astype(F32) for r in refs[:-1])


def per_device(features, tile_values, tile_rows, tile_cols, tile_counts, weight, cotangent):
    nodes = lax.axis_size("node")
    feat = lax.axis_size("feat")
    column = nodes // 2
    width, local = features.shape
    wide = weight.shape[0]
    side = tile_values.shape[1]
    shape = jax.ShapeDtypeStruct
    totals = (local // side, width, side)

    own_across = swapped(features, "node", 1)
    pieces = [swapped(features, "node", 2 * k) for k in range(1, column)]
    masks = shape((tile_values.shape[0], local // side, 16, side), BF16)
    tiles = call(
        prepare,
        [
            pltpu.with_memory_space_constraint(x, pltpu.HBM)
            for x in (tile_rows.T, tile_cols.T, tile_counts, tile_values)
        ],
        [shape(tile_values.shape, BF16), masks, masks],
        [pltpu.SemaphoreType.DMA],
        spec=pl.BlockSpec(memory_space=pltpu.HBM),
    )
    *pieces, own_across, t0, t1, t2 = lax.optimization_barrier((*pieces, own_across, *tiles))
    tiles = (t0, t1, t2)
    (pieces,) = call(stack, pieces, [shape((column - 1, width, local), BF16)])
    far_pieces = swapped(pieces, "node", 1)
    cots = gather_feat(cotangent)
    (near,) = call(
        forward_near, [*tiles, features, pieces, own_across], [shape(totals, F32)]
    )
    (aggregated,) = call(
        forward_far,
        [*tiles, far_pieces, near],
        [shape((width, local), BF16)],
        [pltpu.VMEM(totals, F32)],
    )
    aggs = gather_feat(aggregated)
    activated, grads, mine, dpre, sent = call(
        functools.partial(middle, feat=feat),
        [*tiles, weight, *aggs, *cots],
        [
            shape((wide, side), BF16),
            shape((width, local), BF16),
            shape((wide // 2, local), BF16),
            shape((wide, local), BF16),
            shape((column * width, local), BF16),
        ],
        [pltpu.VMEM((wide, local), BF16)],
    )
    got = swapped(sent, "node", 1)
    near_grads, weight_part = call(
        backward_near,
        [*tiles, grads, mine, dpre],
        [shape((column * width, local), F32), shape((wide // 2, wide), BF16)],
        cost=LARGE,
    )
    parts = [weight_part] + [swapped(weight_part, "node", 2 * k) for k in range(1, column)]
    own, *chunks = call(
        add_pair,
        [near_grads, got],
        [shape((width, local), F32)] + [shape((width, local), BF16)] * (column - 1),
        cost=SMALL,
    )
    arrived = [swapped(c, "node", 2 * k) for k, c in enumerate(chunks, 1)]
    *parts, _ = lax.optimization_barrier((*parts, chunks[0]))
    (part,) = call(sum_weights, parts, [shape((wide // 2, wide), BF16)], cost=SMALL)
    other = swapped(part, "node", 1)
    (column_sum,) = call(
        add_column, [own, *arrived], [shape((width, local), F32)], cost=LARGE
    )
    other, column_sum = lax.optimization_barrier((other, column_sum))
    (half,) = call(sum_weights, [part, other], [shape((wide // 2, wide), F32)], cost=SMALL)
    other_half = swapped(half, "feat", 1)
    activated, grad_weight, gradient = call(
        finish,
        [activated, half, other_half, column_sum],
        [
            shape((wide, side), BF16),
            shape((wide, wide), F32),
            shape((width, local), F32),
        ],
        cost=SMALL,
    )
    return (activated, grad_weight, gradient)


def solution(mesh):
    placed = (
        P("feat", "node"),
        P("node", None, None),
        P("node", None),
        P("node", None),
        P("node"),
        P(),
        P(None, ("node", "feat")),
    )
    return jax.shard_map(
        per_device,
        mesh=mesh,
        in_specs=placed,
        out_specs=(P(None, ("node", "feat")), P(), P("feat", "node")),
        check_vma=False,
    )
```

```python
import functools

import jax
import jax.numpy as jnp
from jax import lax
from jax.experimental import pallas as pl
from jax.experimental.pallas import tpu as pltpu
from jax.sharding import PartitionSpec as P

BF16 = jnp.bfloat16
F32 = jnp.float32
SMEM = pl.BlockSpec(memory_space=pltpu.SMEM)
VMEM = pl.BlockSpec(memory_space=pltpu.VMEM)
LARGE = pl.CostEstimate(flops=10**10, transcendentals=0, bytes_accessed=1 << 20)
SMALL = pl.CostEstimate(flops=1 << 10, transcendentals=0, bytes_accessed=1 << 10)


def swapped(x, axis, mask):
    return lax.ppermute(x, axis, [(i, i ^ mask) for i in range(lax.axis_size(axis))])


def dot(a, b, dims):
    return lax.dot_general(a, b, (dims, ((), ())), preferred_element_type=F32)


def each(count, body):
    if count <= 8:
        for k in range(count):
            body(k)
    else:

        def step(k, carry):
            body(k)
            return carry

        lax.fori_loop(0, count, step, 0)


def lanes(block, side):
    start = block * side
    return pl.ds(start if isinstance(start, int) else pl.multiple_of(start, side), side)


def tree_sum(terms):
    while len(terms) > 1:
        terms = [a + b for a, b in zip(terms[::2], terms[1::2])]
    return terms[0]


def call(body, inputs, outputs, scratch=(), cost=None, spec=VMEM):
    scalars = sum(1 for x in inputs if x.dtype == jnp.int32)
    held = sum(x.size * x.dtype.itemsize for x in [*inputs, *outputs])
    return pl.pallas_call(
        body,
        in_specs=[SMEM] * scalars + [spec] * (len(inputs) - scalars),
        out_specs=[VMEM] * len(outputs),
        out_shape=list(outputs),
        scratch_shapes=list(scratch),
        cost_estimate=cost,
        compiler_params=pltpu.CompilerParams(vmem_limit_bytes=2 * held + (8 << 20)),
    )(*inputs)


def prepare(rows, cols, counts, source, values, row_masks, col_masks, arrival):
    copy = pltpu.make_async_copy(source, values, arrival)
    copy.start()
    slots = rows.shape[0]
    shape = row_masks.shape[2:]

    def one(k):
        for slot in range(slots):
            live = slot < counts[k]
            for ids, masks in ((rows, row_masks), (cols, col_masks)):
                block = jnp.full(shape, jnp.where(live, ids[slot, k], -1), jnp.int32)
                for b in range(masks.shape[1]):
                    masks[k * slots + slot, b] = jnp.where(block == b, 1.0, 0.0).astype(BF16)

    each(rows.shape[1], one)
    copy.wait()


def tile_sums(values, pick, place, piece, pair, transposed):
    blocks = pick.shape[1]
    slots = values.shape[0] // lax.axis_size("node")
    side = values.shape[1]
    high = pick.shape[2]
    loaded = [piece[:, b * side : (b + 1) * side] for b in range(blocks)]
    fold = (-1, high, side)
    sums = [[] for _ in range(blocks)]
    for slot in range(slots):
        at = pair * slots + slot
        chosen = tree_sum([loaded[b].reshape(fold) * pick[at, b] for b in range(blocks)])
        chosen = chosen.reshape(loaded[0].shape)
        product = dot(chosen, values[at], ((1,), (1 if transposed else 0,))).reshape(fold)
        for b in range(blocks):
            sums[b].append(product * place[at, b].astype(F32))
    return [tree_sum(s).reshape(loaded[0].shape) for s in sums]


def forward_near(values, row_masks, col_masks, first, rest, across, totals):
    own = lax.axis_index("node")

    def one(k, piece):
        sums = tile_sums(values, col_masks, row_masks, piece, own ^ k, True)
        for r, part in enumerate(sums):
            totals[r] = part if piece is first else totals[r] + part

    one(0, first)
    one(1, across)
    each(rest.shape[0], lambda k: one(2 * k + 2, rest.at[k]))


def forward_far(values, row_masks, col_masks, rest, near, out, totals):
    own = lax.axis_index("node") ^ 1
    side = values.shape[1]
    totals[...] = near[...]

    def one(k):
        pair = own ^ (2 * k + 2)
        sums = tile_sums(values, col_masks, row_masks, rest.at[k], pair, True)
        for r, part in enumerate(sums):
            totals[r] += part

    each(rest.shape[0], one)
    for r in range(totals.shape[0]):
        out[:, r * side : (r + 1) * side] = totals[r].astype(BF16)


def add_backward(values, row_masks, col_masks, grads, out, flip, first):
    own = lax.axis_index("node") ^ flip
    width = grads.shape[0]
    side = values.shape[1]

    def one(k):
        sums = tile_sums(values, row_masks, col_masks, grads, own ^ (2 * (k + first)), False)
        for c, part in enumerate(sums):
            out[lanes(k, width), c * side : (c + 1) * side] = part.astype(out.dtype)

    each(out.shape[0] // width, one)


def gather_feat(x):
    far = [swapped(x, "feat", m) for m in range(2, lax.axis_size("feat"), 2)]
    held = []
    for piece in [x, *far]:
        held += [piece, swapped(piece, "feat", 1)]
    return held


def stack(*refs):
    pieces, out = refs[:-1], refs[-1]
    for k, piece in enumerate(pieces):
        out[k] = piece[...]


def middle(values, row_masks, col_masks, weight, *refs, feat):
    aggs, cots = refs[:feat], refs[feat : 2 * feat]
    activated, grads, mine, dpre_full, sent_own, sent, agg_full = refs[2 * feat :]
    index = lax.axis_index("feat")
    width, local = aggs[0].shape
    side = cots[0].shape[1]
    for m in range(feat):
        agg_full[lanes(index ^ m, width), :] = aggs[m][...]
    for m in range(feat):
        at = lanes(index ^ m, side)
        pre = dot(weight[...], agg_full[:, at], ((0,), (0,)))
        sigma = 1.0 / (1.0 + jnp.exp(-pre))
        if m == 0:
            activated[...] = (pre * sigma).astype(BF16)
        dpre = cots[m][...].astype(F32) * sigma * (1.0 + pre * (1.0 - sigma))
        dpre_full[:, at] = dpre.astype(BF16)
    dpre_all = dpre_full[...]
    grads[...] = dot(weight[lanes(index, width), :], dpre_all, ((1,), (0,))).astype(BF16)
    mine[...] = agg_full[lanes(index & 1, mine.shape[0]), :]
    add_backward(values, row_masks, col_masks, grads, sent, 1, 1)
    add_backward(values, row_masks, col_masks, grads, sent_own, 1, 0)


def backward_near(values, row_masks, col_masks, grads, mine, dpre, out, weight_part):
    weight_part[...] = dot(mine[...], dpre[...], ((1,), (1,))).astype(BF16)
    add_backward(values, row_masks, col_masks, grads, out, 0, 0)


def add_weights(one, other, out):
    out[...] = (one[...].astype(F32) + other[...].astype(F32)).astype(BF16)


def sum_weights(*refs):
    refs[-1][...] = tree_sum([r[...].astype(F32) for r in refs[:-1]]).astype(refs[-1].dtype)


def add_pair(near, got, *sent):
    width = sent[0].shape[0]
    for k, out in enumerate(sent):
        rows = slice(k * width, (k + 1) * width)
        out[...] = (near[(k + 1) * width : (k + 2) * width] + got[rows].astype(F32)).astype(BF16)


def finish(activated, core, part, across, diagonal, column_sum, *outs):
    activated_out, weight_out, gradient = outs
    activated_out[...] = activated[...]
    own = lax.axis_index("feat") & 1
    rows = part.shape[0]
    weight_out[lanes(own, rows), :] = part[...].astype(F32) + across[...].astype(F32)
    weight_out[lanes(own ^ 1, rows), :] = core[...].astype(F32) + diagonal[...].astype(F32)
    gradient[...] = column_sum[...]


def add_column(near, *refs):
    width = refs[0].shape[0]
    refs[-1][...] = near[:width] + sum(r[...].astype(F32) for r in refs[:-1])


def per_device(features, tile_values, tile_rows, tile_cols, tile_counts, weight, cotangent):
    nodes = lax.axis_size("node")
    feat = lax.axis_size("feat")
    column = nodes // 2
    width, local = features.shape
    wide = weight.shape[0]
    side = tile_values.shape[1]
    shape = jax.ShapeDtypeStruct
    totals = (local // side, width, side)

    own_across = swapped(features, "node", 1)
    pieces = [swapped(features, "node", 2 * k) for k in range(1, column)]
    masks = shape((tile_values.shape[0], local // side, 16, side), BF16)
    tiles = call(
        prepare,
        [
            pltpu.with_memory_space_constraint(x, pltpu.HBM)
            for x in (tile_rows.T, tile_cols.T, tile_counts, tile_values)
        ],
        [shape(tile_values.shape, BF16), masks, masks],
        [pltpu.SemaphoreType.DMA],
        spec=pl.BlockSpec(memory_space=pltpu.HBM),
    )
    *pieces, own_across, t0, t1, t2 = lax.optimization_barrier((*pieces, own_across, *tiles))
    tiles = (t0, t1, t2)
    (pieces,) = call(stack, pieces, [shape((column - 1, width, local), BF16)])
    far_pieces = swapped(pieces, "node", 1)
    cots = gather_feat(cotangent)
    (near,) = call(
        forward_near, [*tiles, features, pieces, own_across], [shape(totals, F32)]
    )
    (aggregated,) = call(
        forward_far,
        [*tiles, far_pieces, near],
        [shape((width, local), BF16)],
        [pltpu.VMEM(totals, F32)],
    )
    aggs = gather_feat(aggregated)
    activated, grads, mine, dpre, sent_own, sent = call(
        functools.partial(middle, feat=feat),
        [*tiles, weight, *aggs, *cots],
        [
            shape((wide, side), BF16),
            shape((width, local), BF16),
            shape((wide // 2, local), BF16),
            shape((wide, local), BF16),
            shape((width, local), BF16),
            shape(((column - 1) * width, local), BF16),
        ],
        [pltpu.VMEM((wide, local), BF16)],
    )
    got = swapped(sent, "node", 1)
    near_grads, weight_part = call(
        backward_near,
        [*tiles, grads, mine, dpre],
        [shape((column * width, local), F32), shape((wide // 2, wide), BF16)],
        cost=LARGE,
    )
    parts = [weight_part] + [swapped(weight_part, "node", 2 * k) for k in range(1, column)]
    chunks = call(
        add_pair,
        [near_grads, got],
        [shape((width, local), BF16)] * (column - 1),
        cost=SMALL,
    )
    arrived = [swapped(c, "node", 2 * k) for k, c in enumerate(chunks, 1)]
    sent_own, _ = lax.optimization_barrier((sent_own, chunks[0]))
    across_own = swapped(sent_own, "node", 1)
    ordered = lax.optimization_barrier(
        (parts[0], *[parts[k] for k in (1, 3, 2)], chunks[0])
    )
    parts = [ordered[0], *[ordered[k] for k in (1, 3, 2)]]
    (part,) = call(sum_weights, parts, [shape((wide // 2, wide), BF16)], cost=SMALL)
    core = swapped(part, "feat", 1)
    across = swapped(part, "node", 1)
    every = range(nodes * feat)
    diagonal = lax.ppermute(part, ("node", "feat"), [(i, i ^ (feat + 1)) for i in every])
    (column_sum,) = call(
        add_column, [near_grads, arrived[0], across_own, *arrived[1:]], [shape((width, local), F32)], cost=LARGE
    )
    core, diagonal, across, column_sum = lax.optimization_barrier(
        (core, diagonal, across, column_sum)
    )
    activated, grad_weight, gradient = call(
        finish,
        [activated, core, part, across, diagonal, column_sum],
        [
            shape((wide, side), BF16),
            shape((wide, wide), F32),
            shape((width, local), F32),
        ],
        cost=SMALL,
    )
    return (activated, grad_weight, gradient)


def solution(mesh):
    placed = (
        P("feat", "node"),
        P("node", None, None),
        P("node", None),
        P("node", None),
        P("node"),
        P(),
        P(None, ("node", "feat")),
    )
    return jax.shard_map(
        per_device,
        mesh=mesh,
        in_specs=placed,
        out_specs=(P(None, ("node", "feat")), P(), P("feat", "node")),
        check_vma=False,
    )
```

```python
import functools

import jax
import jax.numpy as jnp
from jax import lax
from jax.experimental import pallas as pl
from jax.experimental.pallas import tpu as pltpu
from jax.sharding import PartitionSpec as P

BF16 = jnp.bfloat16
F32 = jnp.float32
SMEM = pl.BlockSpec(memory_space=pltpu.SMEM)
VMEM = pl.BlockSpec(memory_space=pltpu.VMEM)
LARGE = pl.CostEstimate(flops=10**10, transcendentals=0, bytes_accessed=1 << 20)
SMALL = pl.CostEstimate(flops=1 << 10, transcendentals=0, bytes_accessed=1 << 10)


def swapped(x, axis, mask):
    return lax.ppermute(x, axis, [(i, i ^ mask) for i in range(lax.axis_size(axis))])


def dot(a, b, dims):
    return lax.dot_general(a, b, (dims, ((), ())), preferred_element_type=F32)


def each(count, body):
    if count <= 8:
        for k in range(count):
            body(k)
    else:

        def step(k, carry):
            body(k)
            return carry

        lax.fori_loop(0, count, step, 0)


def lanes(block, side):
    start = block * side
    return pl.ds(start if isinstance(start, int) else pl.multiple_of(start, side), side)


def tree_sum(terms):
    while len(terms) > 1:
        terms = [a + b for a, b in zip(terms[::2], terms[1::2])]
    return terms[0]


def call(body, inputs, outputs, scratch=(), cost=None, spec=VMEM):
    scalars = sum(1 for x in inputs if x.dtype == jnp.int32)
    held = sum(x.size * x.dtype.itemsize for x in [*inputs, *outputs])
    return pl.pallas_call(
        body,
        in_specs=[SMEM] * scalars + [spec] * (len(inputs) - scalars),
        out_specs=[VMEM] * len(outputs),
        out_shape=list(outputs),
        scratch_shapes=list(scratch),
        cost_estimate=cost,
        compiler_params=pltpu.CompilerParams(vmem_limit_bytes=2 * held + (8 << 20)),
    )(*inputs)


def prepare(rows, cols, counts, source, values, row_masks, col_masks, arrival):
    copy = pltpu.make_async_copy(source, values, arrival)
    copy.start()
    slots = rows.shape[0]
    shape = row_masks.shape[2:]

    def one(k):
        for slot in range(slots):
            live = slot < counts[k]
            for ids, masks in ((rows, row_masks), (cols, col_masks)):
                block = jnp.full(shape, jnp.where(live, ids[slot, k], -1), jnp.int32)
                for b in range(masks.shape[1]):
                    masks[k * slots + slot, b] = jnp.where(block == b, 1.0, 0.0).astype(BF16)

    each(rows.shape[1], one)
    copy.wait()


def tile_sums(values, pick, place, piece, pair, transposed):
    blocks = pick.shape[1]
    slots = values.shape[0] // lax.axis_size("node")
    side = values.shape[1]
    high = pick.shape[2]
    loaded = [piece[:, b * side : (b + 1) * side] for b in range(blocks)]
    fold = (-1, high, side)
    sums = [[] for _ in range(blocks)]
    for slot in range(slots):
        at = pair * slots + slot
        chosen = tree_sum([loaded[b].reshape(fold) * pick[at, b] for b in range(blocks)])
        chosen = chosen.reshape(loaded[0].shape)
        product = dot(chosen, values[at], ((1,), (1 if transposed else 0,))).reshape(fold)
        for b in range(blocks):
            sums[b].append(product * place[at, b].astype(F32))
    return [tree_sum(s).reshape(loaded[0].shape) for s in sums]


def forward_near(values, row_masks, col_masks, first, rest, across, totals):
    own = lax.axis_index("node")

    def one(k, piece):
        sums = tile_sums(values, col_masks, row_masks, piece, own ^ k, True)
        for r, part in enumerate(sums):
            totals[r] = part if piece is first else totals[r] + part

    one(0, first)
    one(1, across)
    each(rest.shape[0], lambda k: one(2 * k + 2, rest.at[k]))


def forward_far(values, row_masks, col_masks, rest, near, out, totals):
    own = lax.axis_index("node") ^ 1
    side = values.shape[1]
    totals[...] = near[...]

    def one(k):
        pair = own ^ (2 * k + 2)
        sums = tile_sums(values, col_masks, row_masks, rest.at[k], pair, True)
        for r, part in enumerate(sums):
            totals[r] += part

    each(rest.shape[0], one)
    for r in range(totals.shape[0]):
        out[:, r * side : (r + 1) * side] = totals[r].astype(BF16)


def add_backward(values, row_masks, col_masks, grads, out, flip, first):
    own = lax.axis_index("node") ^ flip
    width = grads.shape[0]
    side = values.shape[1]

    def one(k):
        sums = tile_sums(values, row_masks, col_masks, grads, own ^ (2 * (k + first)), False)
        for c, part in enumerate(sums):
            out[lanes(k, width), c * side : (c + 1) * side] = part.astype(out.dtype)

    each(out.shape[0] // width, one)


def gather_feat(x):
    far = [swapped(x, "feat", m) for m in range(2, lax.axis_size("feat"), 2)]
    held = []
    for piece in [x, *far]:
        held += [piece, swapped(piece, "feat", 1)]
    return held


def stack(*refs):
    pieces, out = refs[:-1], refs[-1]
    for k, piece in enumerate(pieces):
        out[k] = piece[...]


def middle(values, row_masks, col_masks, weight, *refs, feat):
    aggs, cots = refs[:feat], refs[feat : 2 * feat]
    activated, grads, mine, dpre_full, sent, agg_full = refs[2 * feat :]
    index = lax.axis_index("feat")
    width, local = aggs[0].shape
    side = cots[0].shape[1]
    for m in range(feat):
        agg_full[lanes(index ^ m, width), :] = aggs[m][...]
    for m in range(feat):
        at = lanes(index ^ m, side)
        pre = dot(weight[...], agg_full[:, at], ((0,), (0,)))
        sigma = 1.0 / (1.0 + jnp.exp(-pre))
        if m == 0:
            activated[...] = (pre * sigma).astype(BF16)
        dpre = cots[m][...].astype(F32) * sigma * (1.0 + pre * (1.0 - sigma))
        dpre_full[:, at] = dpre.astype(BF16)
    dpre_all = dpre_full[...]
    grads[...] = dot(weight[lanes(index, width), :], dpre_all, ((1,), (0,))).astype(BF16)
    mine[...] = agg_full[lanes(index & 1, mine.shape[0]), :]
    add_backward(values, row_masks, col_masks, grads, sent, 1, 1)


def backward_near(
    values, row_masks, col_masks, grads, mine, dpre, out, weight_part, sent_own
):
    weight_part[...] = dot(mine[...], dpre[...], ((1,), (1,))).astype(BF16)
    add_backward(values, row_masks, col_masks, grads, out, 0, 0)
    add_backward(values, row_masks, col_masks, grads, sent_own, 1, 0)


def add_weights(one, other, out):
    out[...] = (one[...].astype(F32) + other[...].astype(F32)).astype(BF16)


def sum_weights(*refs):
    refs[-1][...] = tree_sum([r[...].astype(F32) for r in refs[:-1]]).astype(refs[-1].dtype)


def add_pair(near, got, *sent):
    width = sent[0].shape[0]
    for k, out in enumerate(sent):
        rows = slice(k * width, (k + 1) * width)
        out[...] = (near[(k + 1) * width : (k + 2) * width] + got[rows].astype(F32)).astype(BF16)


def finish(activated, core, part, across, diagonal, column_sum, *outs):
    activated_out, weight_out, gradient = outs
    activated_out[...] = activated[...]
    own = lax.axis_index("feat") & 1
    rows = part.shape[0]
    weight_out[lanes(own, rows), :] = part[...].astype(F32) + across[...].astype(F32)
    weight_out[lanes(own ^ 1, rows), :] = core[...].astype(F32) + diagonal[...].astype(F32)
    gradient[...] = column_sum[...]


def add_column(near, *refs):
    width = refs[0].shape[0]
    refs[-1][...] = near[:width] + sum(r[...].astype(F32) for r in refs[:-1])


def per_device(features, tile_values, tile_rows, tile_cols, tile_counts, weight, cotangent):
    nodes = lax.axis_size("node")
    feat = lax.axis_size("feat")
    column = nodes // 2
    width, local = features.shape
    wide = weight.shape[0]
    side = tile_values.shape[1]
    shape = jax.ShapeDtypeStruct
    totals = (local // side, width, side)

    own_across = swapped(features, "node", 1)
    pieces = [swapped(features, "node", 2 * k) for k in range(1, column)]
    masks = shape((tile_values.shape[0], local // side, 16, side), BF16)
    tiles = call(
        prepare,
        [
            pltpu.with_memory_space_constraint(x, pltpu.HBM)
            for x in (tile_rows.T, tile_cols.T, tile_counts, tile_values)
        ],
        [shape(tile_values.shape, BF16), masks, masks],
        [pltpu.SemaphoreType.DMA],
        spec=pl.BlockSpec(memory_space=pltpu.HBM),
    )
    *pieces, own_across, t0, t1, t2 = lax.optimization_barrier((*pieces, own_across, *tiles))
    tiles = (t0, t1, t2)
    (pieces,) = call(stack, pieces, [shape((column - 1, width, local), BF16)])
    far_pieces = swapped(pieces, "node", 1)
    cots = gather_feat(cotangent)
    (near,) = call(
        forward_near, [*tiles, features, pieces, own_across], [shape(totals, F32)]
    )
    (aggregated,) = call(
        forward_far,
        [*tiles, far_pieces, near],
        [shape((width, local), BF16)],
        [pltpu.VMEM(totals, F32)],
    )
    aggs = gather_feat(aggregated)
    activated, grads, mine, dpre, sent = call(
        functools.partial(middle, feat=feat),
        [*tiles, weight, *aggs, *cots],
        [
            shape((wide, side), BF16),
            shape((width, local), BF16),
            shape((wide // 2, local), BF16),
            shape((wide, local), BF16),
            shape(((column - 1) * width, local), BF16),
        ],
        [pltpu.VMEM((wide, local), BF16)],
    )
    got = swapped(sent, "node", 1)
    near_grads, weight_part, sent_own = call(
        backward_near,
        [*tiles, grads, mine, dpre],
        [
            shape((column * width, local), F32),
            shape((wide // 2, wide), BF16),
            shape((width, local), BF16),
        ],
        cost=LARGE,
    )
    parts = [weight_part] + [swapped(weight_part, "node", 2 * k) for k in range(1, column)]
    chunks = call(
        add_pair,
        [near_grads, got],
        [shape((width, local), BF16)] * (column - 1),
        cost=SMALL,
    )
    arrived = [swapped(c, "node", 2 * k) for k, c in enumerate(chunks, 1)]
    sent_own, _ = lax.optimization_barrier((sent_own, chunks[0]))
    across_own = swapped(sent_own, "node", 1)
    ordered = lax.optimization_barrier(
        (parts[0], *[parts[k] for k in (3, 1, 2)], chunks[0])
    )
    parts = [ordered[0], *[ordered[k] for k in (2, 3, 1)]]
    (part,) = call(sum_weights, parts, [shape((wide // 2, wide), BF16)], cost=SMALL)
    core = swapped(part, "feat", 1)
    across = swapped(part, "node", 1)
    every = range(nodes * feat)
    diagonal = lax.ppermute(part, ("node", "feat"), [(i, i ^ (feat + 1)) for i in every])
    (column_sum,) = call(
        add_column, [near_grads, arrived[0], across_own, *arrived[1:]], [shape((width, local), F32)], cost=LARGE
    )
    core, diagonal, across, column_sum = lax.optimization_barrier(
        (core, diagonal, across, column_sum)
    )
    activated, grad_weight, gradient = call(
        finish,
        [activated, core, part, across, diagonal, column_sum],
        [
            shape((wide, side), BF16),
            shape((wide, wide), F32),
            shape((width, local), F32),
        ],
        cost=SMALL,
    )
    return (activated, grad_weight, gradient)


def solution(mesh):
    placed = (
        P("feat", "node"),
        P("node", None, None),
        P("node", None),
        P("node", None),
        P("node"),
        P(),
        P(None, ("node", "feat")),
    )
    return jax.shard_map(
        per_device,
        mesh=mesh,
        in_specs=placed,
        out_specs=(P(None, ("node", "feat")), P(), P("feat", "node")),
        check_vma=False,
    )
```

```python
import functools

import jax
import jax.numpy as jnp
from jax import lax
from jax.experimental import pallas as pl
from jax.experimental.pallas import tpu as pltpu
from jax.sharding import PartitionSpec as P

BF16 = jnp.bfloat16
F32 = jnp.float32
SMEM = pl.BlockSpec(memory_space=pltpu.SMEM)
VMEM = pl.BlockSpec(memory_space=pltpu.VMEM)
LARGE = pl.CostEstimate(flops=10**10, transcendentals=0, bytes_accessed=1 << 20)
SMALL = pl.CostEstimate(flops=1 << 10, transcendentals=0, bytes_accessed=1 << 10)


def swapped(x, axis, mask):
    return lax.ppermute(x, axis, [(i, i ^ mask) for i in range(lax.axis_size(axis))])


def dot(a, b, dims):
    return lax.dot_general(a, b, (dims, ((), ())), preferred_element_type=F32)


def each(count, body):
    if count <= 8:
        for k in range(count):
            body(k)
    else:

        def step(k, carry):
            body(k)
            return carry

        lax.fori_loop(0, count, step, 0)


def lanes(block, side):
    start = block * side
    return pl.ds(start if isinstance(start, int) else pl.multiple_of(start, side), side)


def tree_sum(terms):
    while len(terms) > 1:
        terms = [a + b for a, b in zip(terms[::2], terms[1::2])]
    return terms[0]


def call(body, inputs, outputs, scratch=(), cost=None, spec=VMEM):
    scalars = sum(1 for x in inputs if x.dtype == jnp.int32)
    held = sum(x.size * x.dtype.itemsize for x in [*inputs, *outputs])
    return pl.pallas_call(
        body,
        in_specs=[SMEM] * scalars + [spec] * (len(inputs) - scalars),
        out_specs=[VMEM] * len(outputs),
        out_shape=list(outputs),
        scratch_shapes=list(scratch),
        cost_estimate=cost,
        compiler_params=pltpu.CompilerParams(vmem_limit_bytes=2 * held + (8 << 20)),
    )(*inputs)


def prepare(rows, cols, counts, source, values, row_masks, col_masks, arrival):
    copy = pltpu.make_async_copy(source, values, arrival)
    copy.start()
    slots = rows.shape[0]
    shape = row_masks.shape[2:]

    def one(k):
        for slot in range(slots):
            live = slot < counts[k]
            for ids, masks in ((rows, row_masks), (cols, col_masks)):
                block = jnp.full(shape, jnp.where(live, ids[slot, k], -1), jnp.int32)
                for b in range(masks.shape[1]):
                    masks[k * slots + slot, b] = jnp.where(block == b, 1.0, 0.0).astype(BF16)

    each(rows.shape[1], one)
    copy.wait()


def tile_sums(values, pick, place, piece, pair, transposed):
    blocks = pick.shape[1]
    slots = values.shape[0] // lax.axis_size("node")
    side = values.shape[1]
    high = pick.shape[2]
    loaded = [piece[:, b * side : (b + 1) * side] for b in range(blocks)]
    fold = (-1, high, side)
    sums = [[] for _ in range(blocks)]
    for slot in range(slots):
        at = pair * slots + slot
        chosen = tree_sum([loaded[b].reshape(fold) * pick[at, b] for b in range(blocks)])
        chosen = chosen.reshape(loaded[0].shape)
        product = dot(chosen, values[at], ((1,), (1 if transposed else 0,))).reshape(fold)
        for b in range(blocks):
            sums[b].append(product * place[at, b].astype(F32))
    return [tree_sum(s).reshape(loaded[0].shape) for s in sums]


def forward_near(values, row_masks, col_masks, first, rest, across, totals):
    own = lax.axis_index("node")

    def one(k, piece):
        sums = tile_sums(values, col_masks, row_masks, piece, own ^ k, True)
        for r, part in enumerate(sums):
            totals[r] = part if piece is first else totals[r] + part

    one(0, first)
    one(1, across)
    each(rest.shape[0], lambda k: one(2 * k + 2, rest.at[k]))


def forward_far(values, row_masks, col_masks, rest, near, out, totals):
    own = lax.axis_index("node") ^ 1
    side = values.shape[1]
    totals[...] = near[...]

    def one(k):
        pair = own ^ (2 * k + 2)
        sums = tile_sums(values, col_masks, row_masks, rest.at[k], pair, True)
        for r, part in enumerate(sums):
            totals[r] += part

    each(rest.shape[0], one)
    for r in range(totals.shape[0]):
        out[:, r * side : (r + 1) * side] = totals[r].astype(BF16)


def add_backward(values, row_masks, col_masks, grads, out, flip, first):
    own = lax.axis_index("node") ^ flip
    width = grads.shape[0]
    side = values.shape[1]

    def one(k):
        sums = tile_sums(values, row_masks, col_masks, grads, own ^ (2 * (k + first)), False)
        for c, part in enumerate(sums):
            out[lanes(k, width), c * side : (c + 1) * side] = part.astype(out.dtype)

    each(out.shape[0] // width, one)


def gather_feat(x):
    far = [swapped(x, "feat", m) for m in range(2, lax.axis_size("feat"), 2)]
    held = []
    for piece in [x, *far]:
        held += [piece, swapped(piece, "feat", 1)]
    return held


def stack(*refs):
    pieces, out = refs[:-1], refs[-1]
    for k, piece in enumerate(pieces):
        out[k] = piece[...]


def middle(values, row_masks, col_masks, weight, *refs, feat):
    aggs, cots = refs[:feat], refs[feat : 2 * feat]
    activated, grads, mine, dpre_full, sent_own, sent, agg_full = refs[2 * feat :]
    index = lax.axis_index("feat")
    width, local = aggs[0].shape
    side = cots[0].shape[1]
    for m in range(feat):
        agg_full[lanes(index ^ m, width), :] = aggs[m][...]
    for m in range(feat):
        at = lanes(index ^ m, side)
        pre = dot(weight[...], agg_full[:, at], ((0,), (0,)))
        sigma = 1.0 / (1.0 + jnp.exp(-pre))
        if m == 0:
            activated[...] = (pre * sigma).astype(BF16)
        dpre = cots[m][...].astype(F32) * sigma * (1.0 + pre * (1.0 - sigma))
        dpre_full[:, at] = dpre.astype(BF16)
    dpre_all = dpre_full[...]
    grads[...] = dot(weight[lanes(index, width), :], dpre_all, ((1,), (0,))).astype(BF16)
    mine[...] = agg_full[lanes(index & 1, mine.shape[0]), :]
    add_backward(values, row_masks, col_masks, grads, sent, 1, 1)
    add_backward(values, row_masks, col_masks, grads, sent_own, 1, 0)


def backward_near(values, row_masks, col_masks, grads, mine, dpre, out, weight_part):
    weight_part[...] = dot(mine[...], dpre[...], ((1,), (1,))).astype(BF16)
    add_backward(values, row_masks, col_masks, grads, out, 0, 0)


def add_weights(one, other, out):
    out[...] = (one[...].astype(F32) + other[...].astype(F32)).astype(BF16)


def sum_weights(*refs):
    refs[-1][...] = tree_sum([r[...].astype(F32) for r in refs[:-1]]).astype(refs[-1].dtype)


def add_pair(near, got, *sent):
    width = sent[0].shape[0]
    for k, out in enumerate(sent):
        rows = slice(k * width, (k + 1) * width)
        out[...] = (near[(k + 1) * width : (k + 2) * width] + got[rows].astype(F32)).astype(BF16)


def finish(activated, core, part, across, diagonal, column_sum, *outs):
    activated_out, weight_out, gradient = outs
    activated_out[...] = activated[...]
    own = lax.axis_index("feat") & 1
    rows = part.shape[0]
    weight_out[lanes(own, rows), :] = part[...].astype(F32) + across[...].astype(F32)
    weight_out[lanes(own ^ 1, rows), :] = core[...].astype(F32) + diagonal[...].astype(F32)
    gradient[...] = column_sum[...]


def add_column(near, *refs):
    width = refs[0].shape[0]
    refs[-1][...] = near[:width] + sum(r[...].astype(F32) for r in refs[:-1])


def per_device(features, tile_values, tile_rows, tile_cols, tile_counts, weight, cotangent):
    nodes = lax.axis_size("node")
    feat = lax.axis_size("feat")
    column = nodes // 2
    width, local = features.shape
    wide = weight.shape[0]
    side = tile_values.shape[1]
    shape = jax.ShapeDtypeStruct
    totals = (local // side, width, side)

    own_across = swapped(features, "node", 1)
    pieces = [swapped(features, "node", 2 * k) for k in range(1, column)]
    masks = shape((tile_values.shape[0], local // side, 16, side), BF16)
    tiles = call(
        prepare,
        [
            pltpu.with_memory_space_constraint(x, pltpu.HBM)
            for x in (tile_rows.T, tile_cols.T, tile_counts, tile_values)
        ],
        [shape(tile_values.shape, BF16), masks, masks],
        [pltpu.SemaphoreType.DMA],
        spec=pl.BlockSpec(memory_space=pltpu.HBM),
    )
    *ordered, own_across, t0, t1, t2 = lax.optimization_barrier(
        (*[pieces[k] for k in (1, 0, 2)], own_across, *tiles)
    )
    pieces = [ordered[k] for k in (1, 0, 2)]
    tiles = (t0, t1, t2)
    (pieces,) = call(stack, pieces, [shape((column - 1, width, local), BF16)])
    far_pieces = swapped(pieces, "node", 1)
    cots = gather_feat(cotangent)
    (near,) = call(
        forward_near, [*tiles, features, pieces, own_across], [shape(totals, F32)]
    )
    (aggregated,) = call(
        forward_far,
        [*tiles, far_pieces, near],
        [shape((width, local), BF16)],
        [pltpu.VMEM(totals, F32)],
    )
    aggs = gather_feat(aggregated)
    activated, grads, mine, dpre, sent_own, sent = call(
        functools.partial(middle, feat=feat),
        [*tiles, weight, *aggs, *cots],
        [
            shape((wide, side), BF16),
            shape((width, local), BF16),
            shape((wide // 2, local), BF16),
            shape((wide, local), BF16),
            shape((width, local), BF16),
            shape(((column - 1) * width, local), BF16),
        ],
        [pltpu.VMEM((wide, local), BF16)],
    )
    got = swapped(sent, "node", 1)
    near_grads, weight_part = call(
        backward_near,
        [*tiles, grads, mine, dpre],
        [shape((column * width, local), F32), shape((wide // 2, wide), BF16)],
        cost=LARGE,
    )
    parts = [weight_part] + [swapped(weight_part, "node", 2 * k) for k in range(1, column)]
    chunks = call(
        add_pair,
        [near_grads, got],
        [shape((width, local), BF16)] * (column - 1),
        cost=SMALL,
    )
    arrived = [swapped(c, "node", 2 * k) for k, c in enumerate(chunks, 1)]
    sent_own, _ = lax.optimization_barrier((sent_own, chunks[0]))
    across_own = swapped(sent_own, "node", 1)
    ordered = lax.optimization_barrier(
        (parts[0], *[parts[k] for k in (1, 3, 2)], chunks[0])
    )
    parts = [ordered[0], *[ordered[k] for k in (1, 3, 2)]]
    (part,) = call(sum_weights, parts, [shape((wide // 2, wide), BF16)], cost=SMALL)
    core = swapped(part, "feat", 1)
    across = swapped(part, "node", 1)
    every = range(nodes * feat)
    diagonal = lax.ppermute(part, ("node", "feat"), [(i, i ^ (feat + 1)) for i in every])
    (column_sum,) = call(
        add_column, [near_grads, arrived[0], across_own, *arrived[1:]], [shape((width, local), F32)], cost=LARGE
    )
    core, diagonal, across, column_sum = lax.optimization_barrier(
        (core, diagonal, across, column_sum)
    )
    activated, grad_weight, gradient = call(
        finish,
        [activated, core, part, across, diagonal, column_sum],
        [
            shape((wide, side), BF16),
            shape((wide, wide), F32),
            shape((width, local), F32),
        ],
        cost=SMALL,
    )
    return (activated, grad_weight, gradient)


def solution(mesh):
    placed = (
        P("feat", "node"),
        P("node", None, None),
        P("node", None),
        P("node", None),
        P("node"),
        P(),
        P(None, ("node", "feat")),
    )
    return jax.shard_map(
        per_device,
        mesh=mesh,
        in_specs=placed,
        out_specs=(P(None, ("node", "feat")), P(), P("feat", "node")),
        check_vma=False,
    )
```
